32 devices in a mesh: dp: 4 (over y, x), seq: 8 (over z, core).
Axes of the slice: x: 2, y: 2, z: 4, core: 2. Of those that a mesh axis runs over, the one named last changes fastest.
Arguments:
- block_input: bfloat16 [4, 1024, 1024], P('dp', 'seq'), may hold values from -6 to 6
- in_w: bfloat16 [1024, 3072], P(('dp', 'seq')), may hold values from -0.1875 to 0.1875
- out_w: bfloat16 [1024, 1024], P(('dp', 'seq')), may hold values from -0.1875 to 0.1875
- w_gate: bfloat16 [1024, 4608], P(('dp', 'seq')), may hold values from -0.1875 to 0.1875
- w_up: bfloat16 [1024, 4608], P(('dp', 'seq')), may hold values from -0.1875 to 0.1875
- w_down: bfloat16 [4608, 1024], P(('dp', 'seq')), may hold values from -0.125 to 0.125
- gain_mix: bfloat16 [1024], P(('dp', 'seq')), may hold values from 0.099609375 to 1.8984375
- gain_ffn: bfloat16 [1024], P(('dp', 'seq')), may hold values from 0.099609375 to 1.8984375
- conv_taps: bfloat16 [3, 1024], P(None, ('dp', 'seq')), may hold values from -3 to 3
- output_grad: bfloat16 [4, 1024, 1024], P('dp', 'seq'), may hold values from -6 to 6
Outputs:
- block_output: bfloat16 [4, 1024, 1024], P('dp', 'seq')
- input_grad: float32 [4, 1024, 1024], P('dp', 'seq')
- d_in_w: float32 [1024, 3072], P(('dp', 'seq'))
- d_out_w: float32 [1024, 1024], P(('dp', 'seq'))
- d_w_gate: float32 [1024, 4608], P(('dp', 'seq'))
- d_w_up: float32 [1024, 4608], P(('dp', 'seq'))
- d_w_down: float32 [4608, 1024], P(('dp', 'seq'))
- d_gain_mix: float32 [1024], P(('dp', 'seq'))
- d_gain_ffn: float32 [1024], P(('dp', 'seq'))
- d_conv_taps: float32 [3, 1024], P(None, ('dp', 'seq'))
The draws below stay inside these ranges and needn't reach their ends.
All inputs are finite; a program needn't handle non-finite values.
Results may differ from the reference program's by a relative error of at most 0.011.
Values may be sent and summed in bfloat16 or wider, within the bound.
No kernel may reach another device: no remote copies, remote signals or barrier semaphores. Data moves between devices by JAX's collectives and lax.ppermute only.
A program may use at most 192 MiB of HBM per device.

```python
import jax
import jax.numpy as jnp
from jax import lax

D = 1024
FF = 4608
SEQS = 4
LEN = 1024


def block_levels(rng, shape, split, smallest, largest):
    level = 1.0
    for axis_at, parts in split:
        draws = jax.random.uniform(jax.random.fold_in(jax.random.fold_in(rng, 6), axis_at), (parts,), jnp.float32, smallest / len(split), largest / len(split))
        level = level * jnp.repeat(jnp.exp(draws), shape[axis_at] // parts).reshape((-1,) + (1,) * (len(shape) - 1 - axis_at))
    return level


def bell_draw(key, dims, scale, bound, split=(), dtype=jnp.bfloat16):
    values = jax.random.normal(key, dims, jnp.float32) * scale
    if len(split) > 0:
        values = block_levels(key, dims, split, -0.22, 0.18) * values
    return jnp.clip(values, min=-bound, max=bound).astype(dtype)


def setup_inputs(seed: int = 0) -> dict:
    key_of = jax.random.split(jax.random.key(seed), 11)
    block_input = bell_draw(key_of[0], (SEQS, LEN, D), 1.0, 6.0, ((0, 4), (1, 8)))
    in_w = bell_draw(key_of[1], (D, 3 * D), D ** -0.5, 0.1875, ((0, 32),))
    out_w = bell_draw(key_of[2], (D, D), D ** -0.5, 0.1875, ((0, 32),))
    w_gate = bell_draw(key_of[3], (D, FF), D ** -0.5, 0.1875, ((0, 32),))
    w_up = bell_draw(key_of[4], (D, FF), D ** -0.5, 0.1875, ((0, 32),))
    w_down = bell_draw(key_of[5], (FF, D), (FF // 2) ** -0.5, 0.125, ((0, 32),))
    gain_mix = jnp.clip(1.0 + 0.18 * jax.random.normal(key_of[6], (D,), jnp.float32), 0.099609375, 1.8984375).astype(jnp.bfloat16)
    gain_ffn = jnp.clip(1.0 + 0.18 * jax.random.normal(key_of[7], (D,), jnp.float32), 0.099609375, 1.8984375).astype(jnp.bfloat16)
    conv_taps = bell_draw(key_of[8], (3, D), 0.6, 3.0, ((1, 32),))
    output_grad = bell_draw(key_of[9], (SEQS, LEN, D), 1.0, 6.0, ((0, 4), (1, 8)))
    return {"block_input": block_input, "in_w": in_w, "out_w": out_w, "w_gate": w_gate, "w_up": w_up, "w_down": w_down, "gain_mix": gain_mix, "gain_ffn": gain_ffn, "conv_taps": conv_taps, "output_grad": output_grad}


EPS = 1e-05

def norm_fwd(values, gain):
    scale = lax.rsqrt(lax.optimization_barrier(jnp.mean(values * values, -1, keepdims=True)) + EPS)
    return (values * scale * gain, scale)

def norm_bwd(values, scale, gain, grad):
    hat = values * scale
    inner = grad * gain
    dvalues = scale * (inner - hat * lax.optimization_barrier(jnp.mean(inner * hat, -1, keepdims=True)))
    return (dvalues, lax.optimization_barrier(jnp.sum(grad * hat, 0)))

def tdot(left, right):
    return lax.dot_general(left, right, (((0,), (0,)), ((), ())), preferred_element_type=jnp.float32)

def bdot(left, right):
    return lax.dot_general(left, right, (((1,), (1,)), ((), ())), preferred_element_type=jnp.float32)

def block(inputs, grads_in, in_w, out_w, w_gate, w_up, w_down, gain_mix, gain_ffn, conv_taps):
    width = inputs.shape[1]
    length = inputs.shape[0]
    xf = inputs.astype(jnp.float32)
    gmix = gain_mix.astype(jnp.float32)
    gffn = gain_ffn.astype(jnp.float32)
    tapf = conv_taps.astype(jnp.float32)
    h1, s1 = norm_fwd(xf, gmix)
    a1 = h1.astype(jnp.bfloat16)
    proj = jnp.dot(a1, in_w, preferred_element_type=jnp.float32)
    bgate = proj[:, :width]
    cgate = proj[:, width:2 * width]
    value = proj[:, 2 * width:]
    bx = (bgate * value).astype(jnp.bfloat16)
    ext = jnp.concatenate([jnp.zeros((2, width), jnp.bfloat16), bx], 0).astype(jnp.float32)
    conv = tapf[0] * ext[:length] + tapf[1] * ext[1:length + 1] + tapf[2] * ext[2:]
    a2 = (cgate * conv).astype(jnp.bfloat16)
    resid = xf + jnp.dot(a2, out_w, preferred_element_type=jnp.float32)
    h2, s2 = norm_fwd(resid, gffn)
    a3 = h2.astype(jnp.bfloat16)
    gates = jnp.dot(a3, w_gate, preferred_element_type=jnp.float32)
    upper = jnp.dot(a3, w_up, preferred_element_type=jnp.float32)
    sigm = jax.nn.sigmoid(gates)
    active = gates * sigm
    hid = (active * upper).astype(jnp.bfloat16)
    result = (resid + jnp.dot(hid, w_down, preferred_element_type=jnp.float32)).astype(jnp.bfloat16)
    dyf = grads_in.astype(jnp.float32)
    d_down = tdot(hid, grads_in)
    dhid = bdot(grads_in, w_down)
    dgate = (dhid * upper * (sigm * (1.0 + gates * (1.0 - sigm)))).astype(jnp.bfloat16)
    dupper = (dhid * active).astype(jnp.bfloat16)
    d_gate = tdot(a3, dgate)
    d_up = tdot(a3, dupper)
    da3 = bdot(dgate, w_gate) + bdot(dupper, w_up)
    dres, dg_ffn = norm_bwd(resid, s2, gffn, da3)
    dres = dres + dyf
    drb = dres.astype(jnp.bfloat16)
    d_out = tdot(a2, drb)
    da2 = bdot(drb, out_w)
    dcgate = da2 * conv
    dconv = da2 * cgate
    extd = jnp.concatenate([dconv, jnp.zeros((2, width), jnp.float32)], 0)
    dbx = tapf[2] * extd[:length] + tapf[1] * extd[1:length + 1] + tapf[0] * extd[2:]
    dtaps = jnp.stack([lax.optimization_barrier(jnp.sum(dconv * ext[k:k + length], 0)) for k in range(3)], 0)
    dproj = jnp.concatenate([dbx * value, dcgate, dbx * bgate], 1).astype(jnp.bfloat16)
    d_in = tdot(a1, dproj)
    da1 = bdot(dproj, in_w)
    dx1, dg_mix = norm_bwd(xf, s1, gmix, da1)
    dxs = dres + dx1
    return (result, dxs, (d_in, d_out, d_gate, d_up, d_down, dg_mix, dg_ffn, dtaps))

def reference(block_input, in_w, out_w, w_gate, w_up, w_down, gain_mix, gain_ffn, conv_taps, output_grad):
    weights = (in_w, out_w, w_gate, w_up, w_down, gain_mix, gain_ffn, conv_taps)
    zeros = tuple((jnp.zeros(w.shape, jnp.float32) for w in weights))

    def stepper(carry, pair):
        result, dxs, grads = block(pair[0], pair[1], *weights)
        return (tuple((c + g for c, g in zip(carry, grads))), (result, dxs))
    grads, (block_output, input_grad) = lax.scan(stepper, zeros, (block_input, output_grad))
    return (block_output, input_grad, grads[0], grads[1], grads[2], grads[3], grads[4], grads[5], grads[6], grads[7])
```

```python
import functools

import jax
import jax.numpy as jnp
from jax import lax
from jax.experimental import pallas as pl
from jax.experimental.pallas import tpu as pltpu
from jax.sharding import PartitionSpec as P


EPS = 1e-05
BF = jnp.bfloat16
F32 = jnp.float32
SMEM = pl.BlockSpec(memory_space=pltpu.SMEM)
VMEM = pl.BlockSpec(memory_space=pltpu.VMEM)


def dot(left, right):
    return jnp.dot(left, right, preferred_element_type=F32)


def tdot(left, right):
    return lax.dot_general(left, right, (((0,), (0,)), ((), ())), preferred_element_type=F32)


def bdot(left, right):
    return lax.dot_general(left, right, (((1,), (1,)), ((), ())), preferred_element_type=F32)


def normed(values):
    scale = lax.rsqrt(jnp.mean(values * values, -1, keepdims=True) + EPS)
    return values * scale, scale


def norm_bwd(hat, scale, inner):
    return scale * (inner - hat * jnp.mean(inner * hat, -1, keepdims=True))


def after(value, *earlier):
    return lax.optimization_barrier((value,) + earlier)[0]


def chips():
    return lax.axis_size("seq") // 2


def to_chip(block, k):
    return lax.ppermute(block, "seq", [(i, i ^ (2 * k)) for i in range(lax.axis_size("seq"))])


def swap(block):
    return lax.ppermute(block, "seq", [(i, i ^ 1) for i in range(lax.axis_size("seq"))])


def to_row(block, k):
    return lax.ppermute(block, "dp", [(i, i ^ k) for i in range(lax.axis_size("dp"))])


def gather_seq(block, hold=()):
    blocks = [block] + [to_chip(block, k) for k in range(1, chips())]
    blocks = list(after(tuple(blocks), *hold))
    return [b for mine in blocks for b in (mine, swap(mine))]


def gather_dp(block):
    return [block] + [to_row(block, k) for k in range(1, lax.axis_size("dp"))]


def meet(near, far, rows):
    got = swap(far)
    if not isinstance(near, (list, tuple)):
        near = [near[k : k + rows] for k in range(0, near.shape[0], rows)]
    return [n + got[k * rows : (k + 1) * rows].astype(F32) for k, n in enumerate(near)]


def send_seq(met):
    sent = [m.astype(BF) for m in met[1:]]
    total = met[0]
    for k, part in enumerate(sent):
        total = total + to_chip(part, k + 1).astype(F32)
    return total, sent


def send_dp(pieces, hold=()):
    got = tuple(to_row(part, k + 1) for k, part in enumerate(pieces[1:]))
    total = pieces[0]
    for part in after(got, *hold):
        total = total + part.astype(F32)
    return total


def columns_of(weight, parts):
    dp, seq = lax.axis_size("dp"), lax.axis_size("seq")
    rows, columns = weight.shape
    unit = columns // (parts * dp * seq)
    cut = weight.reshape(rows, parts * dp, seq, unit).transpose(2, 0, 1, 3)
    return cut.reshape(seq, rows, parts * dp * unit)


def exchange(pieces):
    return lax.all_to_all(pieces, "seq", 0, 0, tiled=True)


def rows_of(pieces, parts):
    seq, rows, columns = pieces.shape
    unit = columns // (parts * lax.axis_size("dp"))
    back = pieces.reshape(seq, rows, columns // unit, unit).transpose(1, 2, 0, 3)
    return back.reshape(rows, columns * seq).astype(F32)


def call(kernel, out, smem, inputs, scratch=()):
    out_shape = [jax.ShapeDtypeStruct(shape, dtype) for shape, dtype in out]
    return pl.pallas_call(
        kernel,
        out_shape=out_shape,
        in_specs=[SMEM] * len(smem) + [VMEM] * len(inputs),
        out_specs=[VMEM] * len(out),
        scratch_shapes=list(scratch),
    )(*smem, *inputs)


def at(index, rows):
    return pl.ds(pl.multiple_of(index * rows, rows), rows)


def chosen(index, values):
    total = jnp.zeros_like(values[0])
    for i, value in enumerate(values):
        total = jnp.where(index == i, value, total)
    return total


def place(blocks, whole, where):
    rows = blocks[0].shape[0]
    if rows % 8 == 0:
        for j, block in enumerate(blocks):
            whole[at(where[j], rows), :] = block[...]
        return
    for j, block in enumerate(blocks):
        for i in range(len(blocks)):

            @pl.when(where[j] == i)
            def _():
                whole[i * rows : (i + 1) * rows, :] = block[...]


def take(whole, pieces, where):
    rows = pieces[0].shape[0]
    for k, ref in enumerate(pieces):
        if rows % 8 == 0:
            value = whole[at(where[k], rows), :]
        else:
            values = [whole[i * rows : (i + 1) * rows, :] for i in range(len(pieces))]
            value = chosen(where[k], values)
        ref[...] = value.astype(ref.dtype)


def shift_rows(values, steps):
    rows = values.shape[0]
    row = lax.broadcasted_iota(jnp.int32, values.shape, 0)
    kept = row >= steps if steps > 0 else row < rows + steps
    return jnp.where(kept, pltpu.roll(values, steps % rows, 0), 0.0)


def split(refs, *counts):
    start = 0
    for count in counts:
        yield refs[start : start + count]
        start += count


def mixer_parts(proj, taps, chans):
    bgate, cgate, value = proj[:, :chans], proj[:, chans : 2 * chans], proj[:, 2 * chans :]
    bx = (bgate * value).astype(BF).astype(F32)
    bx1, bx2 = shift_rows(bx, 1), shift_rows(bx, 2)
    conv = taps[0:1] * bx2 + taps[1:2] * bx1 + taps[2:3] * bx
    return bgate, cgate, value, bx, bx1, bx2, conv


def put_slots(part, near, far, where, rows):
    for k, ref in enumerate(near):
        ref[...] = part[at(where[2 * k], rows), :]
        far[k * rows : (k + 1) * rows, :] = part[at(where[2 * k + 1], rows), :].astype(BF)


def mixer_kernel(slots, dps, where, dwhere, *refs):
    xs, ins, outs, res = split(refs, slots, dps, dps, 7 + slots // 2 + 2)
    a1, win, wout, proj_ref, a2_ref, gains, taps = res[:7]
    near, far, part = res[7:-2], res[-2], res[-1]
    rows, width = xs[0].shape
    chans = wout.shape[0]
    place(ins, win, dwhere)
    place(outs, wout, dwhere)
    gain = jnp.transpose(win[:, 3 * chans :].astype(F32))[: gains.shape[0]]
    gains[...] = gain
    tap = jnp.transpose(wout[:, width:].astype(F32))[: taps.shape[0]]
    taps[...] = tap
    for j, x in enumerate(xs):
        hat = normed(x[...].astype(F32))[0]
        a1[at(where[j], rows), :] = (hat * gain[0:1]).astype(BF)
    proj = dot(a1[...], win[:, : 3 * chans])
    proj_ref[...] = proj
    _, cgate, _, _, _, _, conv = mixer_parts(proj, tap, chans)
    a2 = (cgate * conv).astype(BF)
    a2_ref[...] = a2
    part[...] = dot(a2, wout[:, :width])
    put_slots(part, near, far, where, rows)


def mixer(where, dwhere, xs, ins, outs):
    rows, width = xs[0].shape
    length = rows * len(xs)
    chans = outs[0].shape[0] * len(outs)
    out = [
        ((length, width), BF),
        ((width, ins[0].shape[1]), BF),
        ((chans, outs[0].shape[1]), BF),
        ((length, 3 * chans), F32),
        ((length, chans), BF),
        ((8, width), F32),
        ((8, chans), F32),
    ]
    out += [((rows, width), F32)] * (len(xs) // 2) + [((length // 2, width), BF)]
    kernel = functools.partial(mixer_kernel, len(xs), len(ins))
    res = call(kernel, out, [where, dwhere], [*xs, *ins, *outs], [pltpu.VMEM((length, width), F32)])
    return res[:5], res[5], res[6], res[7:-1], res[-1]


def mixer_bwd_kernel(slots, where, taps, win, wout, proj_ref, *refs):
    gs, res = split(refs, slots, slots // 2 + 5)
    near, far = res[: slots // 2], res[slots // 2]
    drb, dproj_ref, lines_ref, part = res[1 + slots // 2 :]
    rows, width = gs[0].shape
    chans = wout.shape[0]
    place(gs, drb, where)
    tap = taps[...]
    bgate, cgate, value, bx, bx1, bx2, conv = mixer_parts(proj_ref[...], tap, chans)
    da2 = bdot(drb[...], wout[:, :width])
    dconv = da2 * cgate
    dbx = tap[2:3] * dconv + tap[1:2] * shift_rows(dconv, -1) + tap[0:1] * shift_rows(dconv, -2)
    dproj = jnp.concatenate([dbx * value, da2 * conv, dbx * bgate], -1).astype(BF)
    dproj_ref[...] = dproj
    part[...] = bdot(dproj, win[:, : 3 * chans])
    put_slots(part, near, far, where, rows)
    lines_ref[...] = jnp.zeros_like(lines_ref)
    for k, v in enumerate((bx2, bx1, bx)):
        lines_ref[k : k + 1, :] = jnp.sum(dconv * v, 0, keepdims=True)


def mixer_grads_kernel(dps, dwhere, a1, a2, drb, dproj, lines, *refs):
    d_outs, d_ins, (d_out, d_in) = split(refs, dps, dps, 2)
    width = drb.shape[1]
    d_in[...] = tdot(a1[...], dproj[...])
    take(d_in, d_ins, dwhere)
    d_out[:, :width] = tdot(a2[...], drb[...])
    d_out[:, width:] = jnp.transpose(lines[...])
    take(d_out, d_outs, dwhere)


def pieces_of(shape, dps):
    return [(shape, F32)] + [(shape, BF)] * (dps - 1)


def mixer_bwd(where, taps, saved, gs):
    _, win, wout, proj, a2 = saved
    rows, width = gs[0].shape
    length, chans = a2.shape
    out = [((rows, width), F32)] * (len(gs) // 2) + [((length // 2, width), BF)]
    out += [((length, width), BF), ((length, 3 * chans), BF), ((128, chans), F32)]
    kernel = functools.partial(mixer_bwd_kernel, len(gs))
    scratch = [pltpu.VMEM((length, width), F32)]
    res = call(kernel, out, [where], [taps, win, wout, proj, *gs], scratch)
    return res[:-4], res[-4], res[-3:]


def mixer_grads(dwhere, saved, more):
    a1, _, wout, _, a2 = saved
    drb, dproj, lines = more
    dps = dwhere.shape[0]
    (width, chans), wide = (a1.shape[1], a2.shape[1]), wout.shape[1]
    out = pieces_of((chans // dps, wide), dps) + pieces_of((width // dps, 3 * chans), dps)
    scratch = [pltpu.VMEM((chans, wide), F32), pltpu.VMEM((width, 3 * chans), F32)]
    kernel = functools.partial(mixer_grads_kernel, dps)
    res = call(kernel, out, [dwhere], [a1, a2, drb, dproj, lines], scratch)
    return res[:dps], res[dps:]


def ffn_kernel(slots, dps, dwhere, *refs):
    xs, gs, wgus, wds, res = split(refs, slots, slots, dps, dps, 10)
    fed_near, fed_far, dn_near, dn_far, hid_ref, dgu_ref, wgu, wd, a3s, dys = res
    rows = xs[0].shape[0]
    units = wd.shape[0]
    place(wgus, wgu, dwhere)
    place(wds, wd, dwhere)
    for j in range(slots):
        a3s[j * rows : (j + 1) * rows, :] = xs[j][...]
        dys[j * rows : (j + 1) * rows, :] = gs[j][...]

    def step(k, _):
        two, one = at(k, 2 * rows), at(k, rows)
        both = dot(a3s[two, :], wgu[...])
        gates, upper = both[:, :units], both[:, units:]
        dhid = bdot(dys[two, :], wd[...])
        sigm = jax.nn.sigmoid(gates)
        active = gates * sigm
        hid = (active * upper).astype(BF)
        dgate = (dhid * upper * (sigm * (1.0 + gates * (1.0 - sigm)))).astype(BF)
        dgu = jnp.concatenate([dgate, (dhid * active).astype(BF)], 1)
        hid_ref[two, :] = hid
        dgu_ref[two, :] = dgu
        dn = bdot(dgu, wgu[...])
        dn_near[one, :] = dn[:rows]
        dn_far[one, :] = dn[rows:].astype(BF)
        fed = dot(hid, wd[...])
        fed_near[one, :] = fed[:rows]
        fed_far[one, :] = fed[rows:].astype(BF)
        return 0

    lax.fori_loop(0, slots // 2, step, 0)


def ffn(dwhere, xs, gs, wgus, wds):
    rows, width = xs[0].shape
    half, dps = len(xs) // 2, len(wds)
    units = wds[0].shape[0] * dps
    parts = [((half * rows, width), F32), ((half * rows, width), BF)]
    out = parts + parts + [((2 * half * rows, units), BF), ((2 * half * rows, 2 * units), BF)]
    scratch = [pltpu.VMEM((width, 2 * units), BF), pltpu.VMEM((units, width), BF)]
    scratch += [pltpu.VMEM((2 * half * rows, width), BF)] * 2
    kernel = functools.partial(ffn_kernel, len(xs), dps)
    res = call(kernel, out, [dwhere], [*xs, *gs, *wgus, *wds], scratch)
    return res[:2], res[2:4], res[4:]


def grads_kernel(slots, calls, dps, dwhere, *refs):
    xs, gs, hids, dgus, d_pairs, d_downs, res = split(
        refs, slots, slots, calls, calls, dps, dps, 6
    )
    a3, dys, hid, dgu, d_pair, d_down = res
    for blocks, whole in ((xs, a3), (gs, dys), (hids, hid), (dgus, dgu)):
        start = 0
        for block in blocks:
            whole[start : start + block.shape[0], :] = block[...]
            start += block.shape[0]
    d_pair[...] = tdot(a3[...], dgu[...])
    take(d_pair, d_pairs, dwhere)
    d_down[...] = tdot(hid[...], dys[...])
    take(d_down, d_downs, dwhere)


def grads(dwhere, xs, gs, mids):
    rows, width = xs[0].shape
    length = rows * len(xs)
    units = mids[0][0].shape[1]
    dps = dwhere.shape[0]
    out = pieces_of((width // dps, 2 * units), dps) + pieces_of((units // dps, width), dps)
    scratch = [pltpu.VMEM((length, width), BF)] * 2
    scratch += [pltpu.VMEM((length, units), BF), pltpu.VMEM((length, 2 * units), BF)]
    scratch += [pltpu.VMEM((width, 2 * units), F32), pltpu.VMEM((units, width), F32)]
    kernel = functools.partial(grads_kernel, len(xs), len(mids), dps)
    flat = [m[0] for m in mids] + [m[1] for m in mids]
    res = call(kernel, out, [dwhere], [*xs, *gs, *flat], scratch)
    return res[:dps], res[dps:]


def fill(values, columns):
    return jnp.pad(values, ((0, 0), (0, columns - values.shape[1])))


def shards(
    block_input, in_w, out_w, w_gate, w_up, w_down, gain_mix, gain_ffn, conv_taps, output_grad
):
    seqs, group, width = block_input.shape
    rows = seqs * group
    assert seqs == 1
    chip, core, row = lax.axis_index("seq") // 2, lax.axis_index("seq") % 2, lax.axis_index("dp")
    slot = jnp.arange(lax.axis_size("seq"), dtype=jnp.int32)
    where = 2 * (chip ^ (slot // 2)) + (core ^ (slot % 2))
    dwhere = row ^ jnp.arange(lax.axis_size("dp"), dtype=jnp.int32)

    seq, lanes = lax.axis_size("seq"), 128
    x_rows, g_rows = block_input.reshape(rows, width), output_grad.reshape(rows, width)
    pair = columns_of(jnp.concatenate([w_gate, w_up], 1), 2)
    xs = gather_seq(x_rows, (pair,))
    unit = in_w.shape[0]
    gains = fill(jnp.stack([gain_mix, gain_ffn], 1), lanes)
    cols = jnp.concatenate(
        [columns_of(in_w, 3), jnp.broadcast_to(gains, (seq,) + gains.shape)], 2
    )
    cols = exchange(cols).reshape(seq * unit, -1)
    ins = gather_dp(cols)
    outs = gather_dp(jnp.concatenate([out_w, fill(conv_taps.transpose(1, 0), lanes)], 1))
    wds = gather_dp(w_down)
    pair = exchange(pair)
    wgus = gather_dp(pair.reshape(seq * unit, -1))
    gs = gather_seq(g_rows)

    xf = x_rows.astype(F32)
    hat1, s1 = normed(xf)
    saved, gains, taps, near, far = mixer(where, dwhere, xs, ins, outs)
    gmix, gffn = gains[0:1], gains[1:2]
    resid = xf + send_seq(meet(near, far, rows))[0]
    hat2, s2 = normed(resid)

    a3s = gather_seq((hat2 * gffn).astype(BF))
    first = ffn(dwhere, a3s[:2], gs[:2], wgus, wds)
    later = ffn(dwhere, a3s[2:], gs[2:], wgus, wds)
    met = meet(*first[1], rows) + meet(*later[1], rows)
    da3, _ = send_seq(met)
    gf = g_rows.astype(F32)
    dres = gf + norm_bwd(hat2, s2, da3 * gffn)

    d_pairs, d_downs = grads(dwhere, a3s, gs, (first[2], later[2]))
    drbs = gather_seq(dres.astype(BF))
    met = meet(*first[0], rows) + meet(*later[0], rows)
    fed, _ = send_seq(met)
    result = (resid + fed).astype(BF)
    near, far, more = mixer_bwd(where, taps, saved, drbs)
    d_outs, d_ins = mixer_grads(dwhere, saved, more)
    da1, sent = send_seq(meet(near, far, rows))
    dxs = dres + norm_bwd(hat1, s1, da1 * gmix)

    e_in = send_dp(d_ins)
    d_in = rows_of(exchange(e_in.astype(BF).reshape(seq, unit, -1)), 3)
    d_out = send_dp(d_outs)
    d_out, dtaps = d_out[:, :width], d_out[:, width : width + 3].transpose(1, 0)

    d_down = send_dp(d_downs, sent)
    e_pair = send_dp(d_pairs, sent)
    e_pair = rows_of(exchange(e_pair.astype(BF).reshape(seq, unit, -1)), 2)
    d_gate, d_up = e_pair[:, : w_gate.shape[1]], e_pair[:, w_gate.shape[1] :]
    wsum = jnp.sum(d_gate * w_gate.astype(F32), 1) + jnp.sum(d_up * w_up.astype(F32), 1)
    dg_ffn = wsum / gain_ffn.astype(F32)
    dg_mix = jnp.sum(d_in * in_w.astype(F32), 1) / gain_mix.astype(F32)
    return (
        result.reshape(seqs, group, width),
        dxs.reshape(seqs, group, width),
        d_in,
        d_out,
        d_gate,
        d_up,
        d_down,
        dg_mix,
        dg_ffn,
        dtaps,
    )


def solution(mesh):
    flat = P(("dp", "seq"), None)
    acts = P("dp", "seq", None)
    vec = P(("dp", "seq"))
    taps = P(None, ("dp", "seq"))
    return jax.shard_map(
        shards,
        mesh=mesh,
        in_specs=(acts, flat, flat, flat, flat, flat, vec, vec, taps, acts),
        out_specs=(acts, acts, flat, flat, flat, flat, flat, vec, vec, taps),
        check_vma=False,
    )
```
